32 devices in a mesh: ta: 2 (over core), ha: 2 (over x), wa: 8 (over z, y).
Axes of the slice: x: 2, y: 2, z: 4, core: 2. Of those that a mesh axis runs over, the one named last changes fastest.
Arguments:
- features: bfloat16 [2, 16, 28, 112, 1024], P(None, 'ta', 'ha', 'wa'), may hold values from -6 to 6
- teacher: bfloat16 [2, 16, 28, 112, 1000], P(None, 'ta', 'ha', 'wa'), may hold values from -30 to 750
- head_weight: float32 [1024, 1000], replicated, may hold values from -0.1875 to 0.1875
Outputs:
- feature_grad: bfloat16 [2, 16, 28, 112, 1024], P(None, 'ta', 'ha', 'wa')
- loss: float32 [], replicated
- new_weight: float32 [1024, 1000], P(('ta', 'ha', 'wa'))
The draws below stay inside these ranges and needn't reach their ends.
All inputs are finite; a program needn't handle non-finite values.
Results may differ from the reference program's by a relative error of at most 0.0056.
Values may be sent and summed in bfloat16 or wider, within the bound.
A program may use at most 192 MiB of HBM per device.

```python
import jax
import jax.numpy as jnp
from jax import lax

D = 1024
CLASSES = 1000
BATCH = 2
WW = 14
WV = 28
NT = 16
NH = 28
NW = 112


def draw_teacher(key, part):
    key_noise = jax.random.fold_in(jax.random.fold_in(key, 17), 0)
    shape = (BATCH, NT, NH, NW, CLASSES)
    return jnp.clip(3.0 * jax.random.normal(key_noise, shape, jnp.float32), -18.0, 18.0).astype(jnp.bfloat16)


def strengthened(array, own_key, source, target, parts, factor):
    owner, partner = [(jnp.arange(array.shape[axis_at]) // (array.shape[axis_at] // parts)).reshape([-1 if axis == axis_at else 1 for axis in range(array.ndim)]) for axis_at in (source, target)]
    chosen = jax.random.permutation(own_key, parts)[partner]
    strong = (owner == chosen) | (owner == (partner + parts // 2) % parts)
    return jnp.where(strong, factor * array, array)


def shard_levels(stream_key, extent, shards, least, top_value):
    loudness = 1.0
    for position, blocks in shards:
        draws = jax.random.uniform(jax.random.fold_in(jax.random.fold_in(stream_key, 6), position), (blocks,), jnp.float32, least / len(shards), top_value / len(shards))
        loudness = loudness * jnp.repeat(jnp.exp(draws), extent[position] // blocks).reshape((-1,) + (1,) * (len(extent) - 1 - position))
    return loudness


def centred(key, extent, spread, bound, shards=(), kind=jnp.bfloat16):
    factor_of = shard_levels(key, extent, shards, -0.22, 0.18) if shards else 1.0
    array = jax.random.normal(key, extent, jnp.float32) * spread * factor_of
    return jnp.minimum(jnp.maximum(array, -bound), bound).astype(kind)


def bell_draw_with(stream_key, dims, deviation, limit, pieces, heavy, kind=jnp.bfloat16):
    values = deviation * jax.random.normal(stream_key, dims, jnp.float32)
    if pieces:
        values = values * shard_levels(stream_key, dims, pieces, -0.22, 0.18)
    return jnp.clip(strengthened(values, jax.random.fold_in(stream_key, 3), *heavy), -limit, limit).astype(kind)


def setup_inputs(seed: int = 0) -> dict:
    keys = jax.random.split(jax.random.key(seed), 4)
    return {
        "features": bell_draw_with(keys[0], (BATCH, NT, NH, NW, D), 1.0, 6.0, ((1, 2), (2, 2), (3, 8)), (3, 4, 8, 2.0)),
        "teacher": draw_teacher(jax.random.fold_in(keys[3], 71), 0),
        "head_weight": centred(keys[2], (D, CLASSES), D ** -0.5, 0.1875, (), jnp.float32),
    }


sharpness_divisor = 2.0
learn_rate = 0.1
clip_norm = 1000.0

def pool_axis(values, reduce_dimension):
    width = [(0, 0)] * values.ndim
    width[reduce_dimension] = (1, 1)
    padded = jnp.pad(values, width)
    length = values.shape[reduce_dimension]
    first = lax.slice_in_dim(padded, 0, length, axis=reduce_dimension)
    middle = lax.slice_in_dim(padded, 1, length + 1, axis=reduce_dimension)
    last = lax.slice_in_dim(padded, 2, length + 2, axis=reduce_dimension)
    return first + middle + last

def clip_of(columns):
    return (columns + WV - WW // 2) // WV

def reference(features, teacher, head_weight):
    head_bf = head_weight.astype(jnp.bfloat16)
    blocks_wide = NW // WV
    teacher_padded = jnp.pad(teacher, ((0, 0), (0, 0), (0, 0), (1, 1), (0, 0)))
    frame_ids = jnp.arange(NT, dtype=jnp.int32)
    row_ids = jnp.arange(NH, dtype=jnp.int32)
    frame_count = (3.0 - (frame_ids == 0).astype(jnp.float32) - (frame_ids == NT - 1).astype(jnp.float32)).reshape(1, NT, 1, 1, 1)
    row_count = (3.0 - (row_ids == 0).astype(jnp.float32) - (row_ids == NH - 1).astype(jnp.float32)).reshape(1, 1, NH, 1, 1)

    def one_block(carry, block):
        head_grad, overall_objective, output = carry
        start = (block * WV).astype(jnp.int32)
        feat_block = lax.dynamic_slice_in_dim(features, start, WV, 3)
        teach_block = lax.dynamic_slice_in_dim(teacher_padded, start, WV + 2, 3).astype(jnp.float32)
        columns = start + jnp.arange(WV, dtype=jnp.int32)
        own_clip = clip_of(columns)
        left_ok = ((columns > 0) & (clip_of(columns - 1) == own_clip)).astype(jnp.float32).reshape(1, 1, 1, WV, 1)
        right_ok = ((columns < NW - 1) & (clip_of(columns + 1) == own_clip)).astype(jnp.float32).reshape(1, 1, 1, WV, 1)
        planar = pool_axis(pool_axis(teach_block, 1), 2)
        summed = planar[:, :, :, 0:WV] * left_ok + planar[:, :, :, 1:WV + 1] + planar[:, :, :, 2:WV + 2] * right_ok
        counts = frame_count * row_count * (1.0 + left_ok + right_ok)
        averaged_scores = (summed / counts).reshape(-1, CLASSES)
        feat_rows = feat_block.reshape(-1, D)
        pupil_scores = jnp.dot(feat_rows, head_bf, preferred_element_type=jnp.float32)
        pupil_entropy_terms = jax.nn.log_softmax(pupil_scores / sharpness_divisor, axis=-1)
        mentor_entropy_terms = jax.nn.log_softmax(averaged_scores / sharpness_divisor, axis=-1)
        mentor_likelihoods = jnp.exp(mentor_entropy_terms)
        pupil_likelihoods = jnp.exp(pupil_entropy_terms)
        patch_kullback_leibler = lax.optimization_barrier(jnp.sum(mentor_likelihoods * (mentor_entropy_terms - pupil_entropy_terms), axis=-1))
        overall_objective = overall_objective + sharpness_divisor * sharpness_divisor * jnp.sum(patch_kullback_leibler)
        score_slope = (sharpness_divisor * (pupil_likelihoods - mentor_likelihoods)).astype(jnp.bfloat16)
        feat_grad = lax.dot_general(score_slope, head_bf, (((1,), (1,)), ((), ())), preferred_element_type=jnp.float32)
        feat_grad = feat_grad.astype(jnp.bfloat16).reshape(feat_block.shape)
        output = lax.dynamic_update_slice_in_dim(output, feat_grad, start, 3)
        head_grad = head_grad + lax.dot_general(feat_rows, score_slope, (((0,), (0,)), ((), ())), preferred_element_type=jnp.float32)
        return ((head_grad, overall_objective, output), None)
    start_carry = (jnp.zeros((D, CLASSES), jnp.float32), jnp.zeros((), jnp.float32), jnp.zeros(features.shape, jnp.bfloat16))
    (head_grad, loss, feature_grad), _ = lax.scan(one_block, start_carry, jnp.arange(blocks_wide, dtype=jnp.int32))
    grad_norm = jnp.sqrt(jnp.sum(head_grad * head_grad))
    clip = jnp.minimum(1.0, clip_norm / (grad_norm + 1e-06))
    new_weight = head_weight - learn_rate * clip * head_grad
    return (feature_grad, loss, new_weight)
```

```python
import functools
import math

import jax
import jax.numpy as jnp
from jax import lax
from jax.experimental import pallas as pl
from jax.experimental.pallas import tpu as pltpu
from jax.sharding import PartitionSpec as P

WW = 14
WV = 28
AXES = ("ta", "ha", "wa")

sharpness_divisor = 2.0
learn_rate = 0.1
clip_norm = 1000.0
EXP2_SCALE = math.log2(math.e) / sharpness_divisor


def clip_of(columns):
    return (columns + WV - WW // 2) // WV


def round_up(value, multiple):
    return -(-value // multiple) * multiple


def exchange_halo(teacher):
    batch, frames, rows, columns, classes = teacher.shape
    ta, ha = lax.axis_index("ta"), lax.axis_index("ha")
    swap = [(0, 1), (1, 0)]
    count = lax.axis_size("wa")
    forward = [(i, i + 1) for i in range(count - 1)]
    backward = [(target, source) for source, target in forward]
    frame = jnp.where(ta == 0, teacher[:, -1], teacher[:, 0])
    frame = lax.ppermute(frame, "ta", swap)
    row = jnp.where(ha == 0, teacher[:, :, -1], teacher[:, :, 0])
    frame_row = jnp.where(ha == 0, frame[:, -1], frame[:, 0])
    row = lax.ppermute(jnp.concatenate([row, frame_row[:, None]], 1), "ha", swap)

    def column(at):
        own = jnp.concatenate([teacher[:, :, :, at], frame[:, None, :, at]], 1)
        return jnp.concatenate([own, row[:, :, at][:, :, None]], 2)

    left = lax.ppermute(column(columns - 1), "wa", forward)
    right = lax.ppermute(column(0), "wa", backward)
    return frame, row, left, right


def pool_weights(rows, columns, wide):
    ha, wa = lax.axis_index("ha"), lax.axis_index("wa")
    grid_wide = columns * lax.axis_size("wa")
    out = jnp.arange(rows * wide, dtype=jnp.int32)
    out_row, out_col = out // wide, out % wide
    halo_row = jnp.where(ha == 0, rows, -1)
    own_row = jnp.arange(rows * wide, dtype=jnp.int32) // wide
    own_col = jnp.arange(rows * wide, dtype=jnp.int32) % wide
    edge_rows = jnp.concatenate([jnp.arange(rows, dtype=jnp.int32), halo_row[None]])
    away = 1 << 20
    src_row = jnp.concatenate([own_row, jnp.full((columns,), 1, jnp.int32) * halo_row, edge_rows, edge_rows])
    src_col = jnp.concatenate(
        [
            jnp.where(own_col < columns, own_col, away),
            jnp.arange(columns, dtype=jnp.int32),
            jnp.full((rows + 1,), -1, jnp.int32),
            jnp.full((rows + 1,), columns, jnp.int32),
        ]
    )
    out_at, src_at = wa * columns + out_col, wa * columns + src_col
    near = (jnp.abs(out_row[:, None] - src_row[None]) <= 1) & (jnp.abs(out_col[:, None] - src_col[None]) <= 1)
    inside = (src_at >= 0) & (src_at < grid_wide)
    same = clip_of(out_at)[:, None] == clip_of(src_at)[None]
    weights = near & inside[None] & same & (out_col < columns)[:, None]
    return weights.astype(jnp.bfloat16)


def fused_kernel(
    frames, columns, flags, own, frame, halo, feats, pool, inverse, head, grad_out, head_grad, loss, sums, slopes, feat_keep
):
    batch_at, step = pl.program_id(0), pl.program_id(1)
    _, _, rows, wide, width = feats.shape
    tokens = rows * wide
    classes = head.shape[1]

    def planar(cells_ref_value, halo_value):
        keep = lax.broadcasted_iota(jnp.int32, cells_ref_value.shape, 1) < columns
        cells = jnp.where(keep, cells_ref_value, jnp.zeros_like(cells_ref_value)).reshape(tokens, classes)
        part = jnp.dot(pool[:, :tokens], cells, preferred_element_type=jnp.float32)
        return part + jnp.dot(pool[:, tokens:], halo_value, preferred_element_type=jnp.float32)

    @pl.when((step == 0) & (batch_at == 0))
    def _():
        loss[...] = jnp.zeros_like(loss)

    @pl.when(step == 0)
    def _():
        sums[2] = planar(frame[0], halo[0, frames]) * flags[0]

    @pl.when(step < frames)
    def _():
        sums[lax.rem(step, 3)] = planar(own[0, 0], halo[0, step])

    @pl.when(step == frames)
    def _():
        sums[frames % 3] = planar(frame[0], halo[0, frames]) * flags[1]

    @pl.when(step > 0)
    def _():
        at = step - 1
        keep = lax.broadcasted_iota(jnp.int32, (rows, wide, width), 1) < columns
        features = jnp.where(keep, feats[0, 0], jnp.zeros((rows, wide, width), feats.dtype)).reshape(tokens, width)
        student = jnp.dot(features, head[...], preferred_element_type=jnp.float32)
        pooled = (sums[0] + sums[1] + sums[2]) * inverse[0]
        teach = (pooled - jnp.max(pooled, -1, keepdims=True)) * EXP2_SCALE
        learn = (student - jnp.max(student, -1, keepdims=True)) * EXP2_SCALE
        teach_exp, learn_exp = jnp.exp2(teach), jnp.exp2(learn)
        teach_sum = jnp.sum(teach_exp, -1, keepdims=True)
        learn_sum = jnp.sum(learn_exp, -1, keepdims=True)
        cross = jnp.sum(teach_exp * (teach - learn), -1, keepdims=True)
        kl = math.log(2.0) * cross / teach_sum + jnp.log(learn_sum) - jnp.log(teach_sum)
        valid = lax.rem(lax.broadcasted_iota(jnp.int32, (tokens, 1), 0), wide) < columns
        kl = jnp.sum(jnp.where(valid, kl, 0.0), axis=0, keepdims=True)
        loss[...] += sharpness_divisor * sharpness_divisor * kl
        slope = learn_exp * (sharpness_divisor / learn_sum) - teach_exp * (sharpness_divisor / teach_sum)
        slope = slope.astype(jnp.bfloat16)
        grad = lax.dot_general(slope, head[...], (((1,), (1,)), ((), ())), preferred_element_type=jnp.float32)
        grad_out[0, 0] = grad.astype(grad_out.dtype).reshape(rows, wide, width)
        where = pl.ds(pl.multiple_of((batch_at * frames + at) * tokens, 16), tokens)
        slopes[where] = slope
        feat_keep[where] = features

    @pl.when((step == frames) & (batch_at == pl.num_programs(0) - 1))
    def _():
        chunk = 256

        @pl.loop(0, width // chunk)
        def _(i):
            part = pl.ds(pl.multiple_of(i * chunk, chunk), chunk)
            head_grad[part] = lax.dot_general(
                feat_keep[:, part], slopes[...], (((0,), (0,)), ((), ())), preferred_element_type=jnp.float32
            )


def local(features, teacher, head_weight):
    batch, frames, rows, columns, width = features.shape
    classes = teacher.shape[-1]
    wide = round_up(columns, 16)
    tokens = rows * wide
    ta, ha, wa = (lax.axis_index(axis) for axis in AXES)
    frame, row, left, right = exchange_halo(teacher)
    halo = jnp.concatenate([row, left, right], axis=2)
    pool = pool_weights(rows, columns, wide)
    frame_at = ta * frames + jnp.arange(frames, dtype=jnp.int32)
    row_at = ha * rows + jnp.arange(rows, dtype=jnp.int32)
    column_at = wa * columns + jnp.arange(wide, dtype=jnp.int32)

    def edge_count(position, length):
        return 3.0 - (position == 0).astype(jnp.float32) - (position == length - 1).astype(jnp.float32)

    own_clip = clip_of(column_at)
    left_ok = (column_at > 0) & (clip_of(column_at - 1) == own_clip)
    right_ok = (column_at < columns * lax.axis_size("wa") - 1) & (clip_of(column_at + 1) == own_clip)
    counts = (
        edge_count(frame_at, frames * lax.axis_size("ta"))[:, None, None]
        * edge_count(row_at, rows * lax.axis_size("ha"))[None, :, None]
        * (1.0 + left_ok.astype(jnp.float32) + right_ok.astype(jnp.float32))[None, None]
    )
    inverse = (1.0 / counts).reshape(frames, tokens, 1)
    flags = jnp.stack([(ta == 1), (ta == 0)]).astype(jnp.float32)
    head_bf = head_weight.astype(jnp.bfloat16)
    lag = lambda b, i: (b, jnp.maximum(i - 1, 0), 0, 0, 0)
    whole = lambda b, i: (0, 0)
    feature_grad, local_grad, loss = pl.pallas_call(
        functools.partial(fused_kernel, frames, columns),
        grid=(batch, frames + 1),
        in_specs=[
            pl.BlockSpec(memory_space=pltpu.SMEM),
            pl.BlockSpec((1, 1, rows, wide, classes), lambda b, i: (b, jnp.minimum(i, frames - 1), 0, 0, 0)),
            pl.BlockSpec((1, rows, wide, classes), lambda b, i: (b, 0, 0, 0)),
            pl.BlockSpec((1,) + halo.shape[1:], lambda b, i: (b, 0, 0, 0)),
            pl.BlockSpec((1, 1, rows, wide, width), lag),
            pl.BlockSpec(pool.shape, whole),
            pl.BlockSpec((1, tokens, 1), lambda b, i: (jnp.maximum(i - 1, 0), 0, 0)),
            pl.BlockSpec(head_bf.shape, whole),
        ],
        out_specs=[
            pl.BlockSpec((1, 1, rows, wide, width), lag),
            pl.BlockSpec((width, classes), whole),
            pl.BlockSpec((1, 1), whole),
        ],
        out_shape=[
            jax.ShapeDtypeStruct(features.shape, features.dtype),
            jax.ShapeDtypeStruct((width, classes), jnp.float32),
            jax.ShapeDtypeStruct((1, 1), jnp.float32),
        ],
        scratch_shapes=[
            pltpu.VMEM((3, tokens, classes), jnp.float32),
            pltpu.VMEM((batch * frames * tokens, classes), jnp.bfloat16),
            pltpu.VMEM((batch * frames * tokens, width), jnp.bfloat16),
        ],
        compiler_params=pltpu.CompilerParams(vmem_limit_bytes=60 * 1024 * 1024),
    )(flags, teacher, frame, halo, features, pool, inverse, head_bf)
    owned = width // lax.axis_size(AXES)
    mine = lax.psum_scatter(local_grad, AXES, scatter_dimension=0, tiled=True)
    squares, loss = lax.psum((jnp.sum(mine * mine), loss[0, 0]), AXES)
    clip = jnp.minimum(1.0, clip_norm / (jnp.sqrt(squares) + 1e-06))
    weight_rows = lax.dynamic_slice_in_dim(head_weight, lax.axis_index(AXES) * owned, owned, 0)
    return feature_grad, loss, weight_rows - learn_rate * clip * mine


def solution(mesh):
    assert mesh.shape["ta"] == 2 and mesh.shape["ha"] == 2
    placed = (P(None, "ta", "ha", "wa", None), P(None, "ta", "ha", "wa", None), P())
    return jax.shard_map(
        local,
        mesh=mesh,
        in_specs=placed,
        out_specs=(P(None, "ta", "ha", "wa", None), P(), P(AXES, None)),
        check_vma=False,
    )
```

```python
import functools
import math

import jax
import jax.numpy as jnp
from jax import lax
from jax.experimental import pallas as pl
from jax.experimental.pallas import tpu as pltpu
from jax.sharding import PartitionSpec as P

WW = 14
WV = 28
AXES = ("ta", "ha", "wa")

sharpness_divisor = 2.0
learn_rate = 0.1
clip_norm = 1000.0
EXP2_SCALE = math.log2(math.e) / sharpness_divisor


def clip_of(columns):
    return (columns + WV - WW // 2) // WV


def round_up(value, multiple):
    return -(-value // multiple) * multiple


def exchange_halo(teacher):
    batch, frames, rows, columns, classes = teacher.shape
    ta, ha = lax.axis_index("ta"), lax.axis_index("ha")
    swap = [(0, 1), (1, 0)]
    count = lax.axis_size("wa")
    forward = [(i, i + 1) for i in range(count - 1)]
    backward = [(target, source) for source, target in forward]
    frame = jnp.where(ta == 0, teacher[:, -1], teacher[:, 0])
    frame = lax.ppermute(frame, "ta", swap)
    row = jnp.where(ha == 0, teacher[:, :, -1], teacher[:, :, 0])
    frame_row = jnp.where(ha == 0, frame[:, -1], frame[:, 0])
    row = lax.ppermute(jnp.concatenate([row, frame_row[:, None]], 1), "ha", swap)

    def column(at):
        own = jnp.concatenate([teacher[:, :, :, at], frame[:, None, :, at]], 1)
        return jnp.concatenate([own, row[:, :, at][:, :, None]], 2)

    left = lax.ppermute(column(columns - 1), "wa", forward)
    right = lax.ppermute(column(0), "wa", backward)
    return frame, row, left, right


def pool_weights(rows, columns, wide):
    ha, wa = lax.axis_index("ha"), lax.axis_index("wa")
    grid_wide = columns * lax.axis_size("wa")
    out = jnp.arange(rows * wide, dtype=jnp.int32)
    out_row, out_col = out // wide, out % wide
    halo_row = jnp.where(ha == 0, rows, -1)
    own_row = jnp.arange(rows * wide, dtype=jnp.int32) // wide
    own_col = jnp.arange(rows * wide, dtype=jnp.int32) % wide
    edge_rows = jnp.concatenate([jnp.arange(rows, dtype=jnp.int32), halo_row[None]])
    away = 1 << 20
    src_row = jnp.concatenate([own_row, jnp.full((columns,), 1, jnp.int32) * halo_row, edge_rows, edge_rows])
    src_col = jnp.concatenate(
        [
            jnp.where(own_col < columns, own_col, away),
            jnp.arange(columns, dtype=jnp.int32),
            jnp.full((rows + 1,), -1, jnp.int32),
            jnp.full((rows + 1,), columns, jnp.int32),
        ]
    )
    out_at, src_at = wa * columns + out_col, wa * columns + src_col
    near = (jnp.abs(out_row[:, None] - src_row[None]) <= 1) & (jnp.abs(out_col[:, None] - src_col[None]) <= 1)
    inside = (src_at >= 0) & (src_at < grid_wide)
    same = clip_of(out_at)[:, None] == clip_of(src_at)[None]
    weights = near & inside[None] & same & (out_col < columns)[:, None]
    return weights.astype(jnp.bfloat16)


def fused_kernel(
    frames, columns, flags, own, frame, halo, feats, pool, inverse, head, grad_out, head_grad, loss, sums, slopes, feat_keep
):
    batch_at, step = pl.program_id(0), pl.program_id(1)
    _, _, rows, wide, width = feats.shape
    tokens = rows * wide
    classes = head.shape[1]

    def planar(cells_ref_value, halo_value):
        keep = lax.broadcasted_iota(jnp.int32, cells_ref_value.shape, 1) < columns
        cells = jnp.where(keep, cells_ref_value, jnp.zeros_like(cells_ref_value)).reshape(tokens, classes)
        part = jnp.dot(pool[:, :tokens], cells, preferred_element_type=jnp.float32)
        return part + jnp.dot(pool[:, tokens:], halo_value, preferred_element_type=jnp.float32)

    @pl.when((step == 0) & (batch_at == 0))
    def _():
        loss[...] = jnp.zeros_like(loss)

    @pl.when(step == 0)
    def _():
        sums[2] = planar(frame[0], halo[0, frames]) * flags[0]

    @pl.when(step < frames)
    def _():
        sums[lax.rem(step, 3)] = planar(own[0, 0], halo[0, step])

    @pl.when(step == frames)
    def _():
        sums[frames % 3] = planar(frame[0], halo[0, frames]) * flags[1]

    @pl.when(step > 0)
    def _():
        at = step - 1
        keep = lax.broadcasted_iota(jnp.int32, (rows, wide, width), 1) < columns
        features = jnp.where(keep, feats[0, 0], jnp.zeros((rows, wide, width), feats.dtype)).reshape(tokens, width)
        student = jnp.dot(features, head[...], preferred_element_type=jnp.float32)
        pooled = (sums[0] + sums[1] + sums[2]) * inverse[0]
        teach = (pooled - jnp.max(pooled, -1, keepdims=True)) * EXP2_SCALE
        learn = (student - jnp.max(student, -1, keepdims=True)) * EXP2_SCALE
        teach_exp, learn_exp = jnp.exp2(teach), jnp.exp2(learn)
        teach_sum = jnp.sum(teach_exp, -1, keepdims=True)
        learn_sum = jnp.sum(learn_exp, -1, keepdims=True)
        cross = jnp.sum(teach_exp * (teach - learn), -1, keepdims=True)
        kl = math.log(2.0) * cross / teach_sum + jnp.log(learn_sum) - jnp.log(teach_sum)
        valid = lax.rem(lax.broadcasted_iota(jnp.int32, (tokens, 1), 0), wide) < columns
        kl = jnp.sum(jnp.where(valid, kl, 0.0), axis=0, keepdims=True)
        loss[...] += sharpness_divisor * sharpness_divisor * kl
        slope = learn_exp * (sharpness_divisor / learn_sum) - teach_exp * (sharpness_divisor / teach_sum)
        slope = slope.astype(jnp.bfloat16)
        grad = lax.dot_general(slope, head[...], (((1,), (1,)), ((), ())), preferred_element_type=jnp.float32)
        grad_out[0, 0] = grad.astype(grad_out.dtype).reshape(rows, wide, width)
        where = pl.ds(pl.multiple_of((batch_at * frames + at) * tokens, 16), tokens)
        slopes[where] = slope
        feat_keep[where] = features

    @pl.when((step == frames) & (batch_at == pl.num_programs(0) - 1))
    def _():
        chunk = 256

        @pl.loop(0, width // chunk)
        def _(i):
            part = pl.ds(pl.multiple_of(i * chunk, chunk), chunk)
            head_grad[part] = lax.dot_general(
                feat_keep[:, part], slopes[...], (((0,), (0,)), ((), ())), preferred_element_type=jnp.float32
            ).astype(head_grad.dtype)


def reduce_kernel(peers, partial, local_loss, weight, new_weight, loss, landed, summed, arrived, stats, stat_in, stat_out, gathered,
                  core_send, core_recv, peer_send, peer_recv, stat_send, stat_recv, pair_sem):
    ta, ha, wa = (lax.axis_index(axis) for axis in AXES)
    per_row = lax.axis_size("wa")
    me = ha * per_row + wa
    other = {"ta": 1 - ta}

    def peer(k):
        return lax.rem(me + k, peers)

    def place(at):
        return {"ha": at // per_row, "wa": lax.rem(at, per_row)}

    barrier = pltpu.get_barrier_semaphore()
    pl.semaphore_signal(barrier, inc=1, device_id=other, device_id_type=pl.DeviceIdType.MESH)

    @pl.loop(1, peers)
    def _(k):
        pl.semaphore_signal(barrier, inc=1, device_id=place(peer(k)), device_id_type=pl.DeviceIdType.MESH)

    pl.semaphore_wait(barrier, peers)

    def to_core(k):
        at = peer(k)
        return pltpu.make_async_remote_copy(
            src_ref=partial.at[1 - ta, at], dst_ref=landed.at[at], send_sem=core_send.at[lax.rem(k, peers)],
            recv_sem=core_recv.at[lax.rem(k, peers)], device_id=other, device_id_type=pl.DeviceIdType.MESH)

    def to_peer(k):
        at = peer(k)
        return pltpu.make_async_remote_copy(
            src_ref=summed.at[at], dst_ref=arrived.at[k], send_sem=peer_send.at[k],
            recv_sem=peer_recv.at[k], device_id=place(at), device_id_type=pl.DeviceIdType.MESH)

    def stat_to(k):
        return pltpu.make_async_remote_copy(
            src_ref=stats, dst_ref=gathered.at[me], send_sem=stat_send.at[k],
            recv_sem=stat_recv.at[k], device_id=place(peer(k)), device_id_type=pl.DeviceIdType.MESH)

    @pl.loop(1, peers + 1)
    def _(k):
        to_core(k).start()

    @pl.loop(1, peers)
    def _(k):
        at = peer(k)
        to_core(k).wait_recv()
        summed[at] = (partial[ta, at].astype(jnp.float32) + landed[at].astype(jnp.float32)).astype(summed.dtype)
        to_peer(k).start()

    to_core(peers).wait_recv()
    new_weight[...] = partial[ta, me].astype(jnp.float32) + landed[me].astype(jnp.float32)

    @pl.loop(1, peers)
    def _(k):
        to_peer(k).wait_recv()
        new_weight[...] += arrived[k].astype(jnp.float32)

    total = new_weight[...]
    squares = jnp.sum(jnp.sum(total * total, axis=1, keepdims=True), axis=0, keepdims=True)
    lane = lax.broadcasted_iota(jnp.int32, stat_out.shape, 1)
    stat_out[...] = jnp.where(lane == 0, squares, local_loss[...])
    pair = pltpu.make_async_remote_copy(
        src_ref=stat_out, dst_ref=stat_in, send_sem=pair_sem.at[0], recv_sem=pair_sem.at[1],
        device_id=other, device_id_type=pl.DeviceIdType.MESH)
    pair.start()
    pair.wait()
    stats[...] = stat_out[...] + stat_in[...]
    gathered[me] = stats[...]

    @pl.loop(1, peers)
    def _(k):
        stat_to(k).start()

    @pl.loop(1, peers)
    def _(k):
        stat_to(k).wait_recv()

    both = jnp.sum(gathered[...], axis=0)
    norm = jnp.sqrt(both[0:1, 0:1])
    loss[...] = both[0:1, 1:2]
    clip = jnp.minimum(1.0, clip_norm / (norm + 1e-06))
    new_weight[...] = weight[...] - learn_rate * clip * new_weight[...]

    @pl.loop(1, peers)
    def _(k):
        to_core(k).wait_send()
        to_peer(k).wait_send()
        stat_to(k).wait_send()

    to_core(peers).wait_send()


def reduce_and_update(local_grad, local_loss, weight_rows):
    owned, classes = weight_rows.shape
    peers = lax.axis_size(("ha", "wa"))
    partial = local_grad.reshape(2, peers, owned, classes)
    vmem = pl.BlockSpec(memory_space=pltpu.VMEM)
    dma = pltpu.SemaphoreType.DMA
    slots = pltpu.VMEM((peers, owned, classes), local_grad.dtype)
    return pl.pallas_call(
        functools.partial(reduce_kernel, peers),
        in_specs=[vmem] * 3,
        out_specs=[vmem] * 2,
        out_shape=[
            jax.ShapeDtypeStruct((owned, classes), jnp.float32),
            jax.ShapeDtypeStruct((1, 1), jnp.float32),
        ],
        scratch_shapes=[slots, slots, slots]
        + [pltpu.VMEM((8, 128), jnp.float32)] * 3
        + [pltpu.VMEM((peers, 8, 128), jnp.float32)]
        + [dma((peers,))] * 6
        + [dma((2,))],
        compiler_params=pltpu.CompilerParams(collective_id=0, has_side_effects=True),
    )(partial, local_loss, weight_rows)


def local(features, teacher, head_weight):
    batch, frames, rows, columns, width = features.shape
    classes = teacher.shape[-1]
    wide = round_up(columns, 16)
    tokens = rows * wide
    ta, ha, wa = (lax.axis_index(axis) for axis in AXES)
    frame, row, left, right = exchange_halo(teacher)
    halo = jnp.concatenate([row, left, right], axis=2)
    pool = pool_weights(rows, columns, wide)
    frame_at = ta * frames + jnp.arange(frames, dtype=jnp.int32)
    row_at = ha * rows + jnp.arange(rows, dtype=jnp.int32)
    column_at = wa * columns + jnp.arange(wide, dtype=jnp.int32)

    def edge_count(position, length):
        return 3.0 - (position == 0).astype(jnp.float32) - (position == length - 1).astype(jnp.float32)

    own_clip = clip_of(column_at)
    left_ok = (column_at > 0) & (clip_of(column_at - 1) == own_clip)
    right_ok = (column_at < columns * lax.axis_size("wa") - 1) & (clip_of(column_at + 1) == own_clip)
    counts = (
        edge_count(frame_at, frames * lax.axis_size("ta"))[:, None, None]
        * edge_count(row_at, rows * lax.axis_size("ha"))[None, :, None]
        * (1.0 + left_ok.astype(jnp.float32) + right_ok.astype(jnp.float32))[None, None]
    )
    inverse = (1.0 / counts).reshape(frames, tokens, 1)
    flags = jnp.stack([(ta == 1), (ta == 0)]).astype(jnp.float32)
    head_bf = head_weight.astype(jnp.bfloat16)
    lag = lambda b, i: (b, jnp.maximum(i - 1, 0), 0, 0, 0)
    whole = lambda b, i: (0, 0)
    feature_grad, local_grad, loss = pl.pallas_call(
        functools.partial(fused_kernel, frames, columns),
        grid=(batch, frames + 1),
        in_specs=[
            pl.BlockSpec(memory_space=pltpu.SMEM),
            pl.BlockSpec((1, 1, rows, wide, classes), lambda b, i: (b, jnp.minimum(i, frames - 1), 0, 0, 0)),
            pl.BlockSpec((1, rows, wide, classes), lambda b, i: (b, 0, 0, 0)),
            pl.BlockSpec((1,) + halo.shape[1:], lambda b, i: (b, 0, 0, 0)),
            pl.BlockSpec((1, 1, rows, wide, width), lag),
            pl.BlockSpec(pool.shape, whole),
            pl.BlockSpec((1, tokens, 1), lambda b, i: (jnp.maximum(i - 1, 0), 0, 0)),
            pl.BlockSpec(head_bf.shape, whole),
        ],
        out_specs=[
            pl.BlockSpec((1, 1, rows, wide, width), lag),
            pl.BlockSpec((width, classes), whole),
            pl.BlockSpec((1, 1), whole),
        ],
        out_shape=[
            jax.ShapeDtypeStruct(features.shape, features.dtype),
            jax.ShapeDtypeStruct((width, classes), jnp.bfloat16),
            jax.ShapeDtypeStruct((1, 1), jnp.float32),
        ],
        scratch_shapes=[
            pltpu.VMEM((3, tokens, classes), jnp.float32),
            pltpu.VMEM((batch * frames * tokens, classes), jnp.bfloat16),
            pltpu.VMEM((batch * frames * tokens, width), jnp.bfloat16),
        ],
        compiler_params=pltpu.CompilerParams(vmem_limit_bytes=60 * 1024 * 1024),
    )(flags, teacher, frame, halo, features, pool, inverse, head_bf)
    owned = width // lax.axis_size(AXES)
    weight_rows = lax.dynamic_slice_in_dim(head_weight, lax.axis_index(AXES) * owned, owned, 0)
    new_weight, loss = reduce_and_update(local_grad, loss, weight_rows)
    return feature_grad, loss[0, 0], new_weight


def solution(mesh):
    assert mesh.shape["ta"] == 2 and mesh.shape["ha"] == 2
    placed = (P(None, "ta", "ha", "wa", None), P(None, "ta", "ha", "wa", None), P())
    return jax.shard_map(
        local,
        mesh=mesh,
        in_specs=placed,
        out_specs=(P(None, "ta", "ha", "wa", None), P(), P(AXES, None)),
        check_vma=False,
    )
```

```python
import functools
import math

import jax
import jax.numpy as jnp
from jax import lax
from jax.experimental import pallas as pl
from jax.experimental.pallas import tpu as pltpu
from jax.sharding import PartitionSpec as P

WW = 14
WV = 28
AXES = ("ta", "ha", "wa")

sharpness_divisor = 2.0
learn_rate = 0.1
clip_norm = 1000.0
EXP2_SCALE = math.log2(math.e) / sharpness_divisor


def clip_of(columns):
    return (columns + WV - WW // 2) // WV


def exchange_halo(teacher):
    batch, rows, columns, frames, classes = teacher.shape
    ta, ha = lax.axis_index("ta"), lax.axis_index("ha")
    swap = [(0, 1), (1, 0)]
    count = lax.axis_size("wa")
    forward = [(i, i + 1) for i in range(count - 1)]
    backward = [(target, source) for source, target in forward]

    def facing_frame(cells):
        facing = lax.broadcasted_iota(jnp.int32, cells.shape, cells.ndim - 2) == jnp.where(ta == 0, frames - 1, 0)
        return jnp.sum(jnp.where(facing, cells, jnp.zeros_like(cells)), axis=-2)

    row = lax.dynamic_slice_in_dim(teacher, jnp.where(ha == 0, rows - 1, 0), 1, 1)
    row = lax.ppermute(row, "ha", swap)
    frame = lax.ppermute(facing_frame(teacher), "ta", swap)
    left = lax.ppermute(jnp.concatenate([teacher[:, :, -1], row[:, :, -1]], 1), "wa", forward)
    right = lax.ppermute(jnp.concatenate([teacher[:, :, 0], row[:, :, 0]], 1), "wa", backward)
    edges = jnp.concatenate([facing_frame(row[:, 0]), facing_frame(left), facing_frame(right)], 1)
    edges = lax.ppermute(edges, "ta", swap)
    frame = jnp.concatenate([frame, edges[:, None, :columns]], 1)
    frame_left = edges[:, columns : columns + rows + 1, None]
    frame_right = edges[:, columns + rows + 1 :, None]
    return row, jnp.concatenate([left, right, frame, frame_left, frame_right], 2)


def pool_weights(columns, frames):
    ta, wa = lax.axis_index("ta"), lax.axis_index("wa")
    grid_wide = columns * lax.axis_size("wa")
    out = jnp.arange(columns * frames, dtype=jnp.int32)
    out_col, out_frame = out // frames, out % frames
    every = jnp.arange(frames, dtype=jnp.int32)
    cols = jnp.arange(columns, dtype=jnp.int32)
    next_frame = jnp.where(ta == 0, frames, -1)
    src_col = jnp.concatenate([out_col, 0 * every - 1, 0 * every + columns, cols, jnp.array([-1, columns], jnp.int32)])
    src_frame = jnp.concatenate([out_frame, every, every, jnp.full((columns + 2,), 1, jnp.int32) * next_frame])
    out_at, src_at = wa * columns + out_col, wa * columns + src_col
    near = (jnp.abs(out_frame[:, None] - src_frame[None]) <= 1) & (jnp.abs(out_col[:, None] - src_col[None]) <= 1)
    inside = (src_at >= 0) & (src_at < grid_wide)
    same = clip_of(out_at)[:, None] == clip_of(src_at)[None]
    return (near & inside[None] & same).astype(jnp.bfloat16)


def fused_kernel(rows, flags, own, halo_row, halo, feats, pool, inverse, head, grad_out, head_grad, loss, sums, slopes, feat_keep):
    step = pl.program_id(0)
    batch, _, columns, frames, width = feats.shape
    per_batch = columns * frames
    tokens = batch * per_batch
    classes = head.shape[1]

    def planar(slot, cells_of, scale=None):
        for b in range(batch):
            cells = jnp.concatenate([cells_of(b).reshape(per_batch, classes), halo[b, 0]], axis=0)
            part = jnp.dot(pool[...], cells, preferred_element_type=jnp.float32)
            sums[slot, b * per_batch : (b + 1) * per_batch] = part if scale is None else part * scale

    @pl.when(step == 0)
    def _():
        loss[...] = jnp.zeros_like(loss)
        planar(rows % 3, lambda b: halo_row[b, 0], flags[0])

    @pl.when((step > 0) & (step <= rows))
    def _():
        planar(lax.rem(step - 1, 3), lambda b: own[b, 0])

    @pl.when(step == rows + 1)
    def _():
        planar(rows % 3, lambda b: halo_row[b, 0], flags[1])

    @pl.when(step > 1)
    def _():
        at = step - 2
        features = feats[...].reshape(tokens, width)
        student = jnp.dot(features, head[...], preferred_element_type=jnp.float32)
        pooled = (sums[0] + sums[1] + sums[2]) * inverse[0]
        teach = (pooled - jnp.max(pooled, -1, keepdims=True)) * EXP2_SCALE
        learn = (student - jnp.max(student, -1, keepdims=True)) * EXP2_SCALE
        teach_exp, learn_exp = jnp.exp2(teach), jnp.exp2(learn)
        teach_sum = jnp.sum(teach_exp, -1, keepdims=True)
        learn_sum = jnp.sum(learn_exp, -1, keepdims=True)
        cross = jnp.sum(teach_exp * (teach - learn), -1, keepdims=True)
        kl = math.log(2.0) * cross / teach_sum + jnp.log(learn_sum) - jnp.log(teach_sum)
        loss[...] += sharpness_divisor * sharpness_divisor * jnp.sum(kl, axis=0, keepdims=True)
        slope = learn_exp * (sharpness_divisor / learn_sum) - teach_exp * (sharpness_divisor / teach_sum)
        slope = slope.astype(jnp.bfloat16)
        grad = lax.dot_general(slope, head[...], (((1,), (1,)), ((), ())), preferred_element_type=jnp.float32)
        grad_out[...] = grad.astype(grad_out.dtype).reshape(grad_out.shape)
        where = pl.ds(pl.multiple_of(at * tokens, 16), tokens)
        slopes[where] = slope
        feat_keep[where] = features

    @pl.when(step == rows + 1)
    def _():
        chunk = 256

        @pl.loop(0, width // chunk)
        def _(i):
            part = pl.ds(pl.multiple_of(i * chunk, chunk), chunk)
            head_grad[part] = lax.dot_general(
                feat_keep[:, part], slopes[...], (((0,), (0,)), ((), ())), preferred_element_type=jnp.float32
            ).astype(head_grad.dtype)


def reduce_kernel(peers, partial, local_loss, weight, new_weight, loss, landed, summed, arrived, stats, stat_in, stat_out, gathered,
                  core_send, core_recv, peer_send, peer_recv, stat_send, stat_recv, pair_sem):
    ta, ha, wa = (lax.axis_index(axis) for axis in AXES)
    per_row = lax.axis_size("wa")
    me = ha * per_row + wa
    other = {"ta": 1 - ta}

    def peer(k):
        return lax.rem(me + k, peers)

    def place(at):
        return {"ha": at // per_row, "wa": lax.rem(at, per_row)}

    barrier = pltpu.get_barrier_semaphore()
    pl.semaphore_signal(barrier, inc=1, device_id=other, device_id_type=pl.DeviceIdType.MESH)

    @pl.loop(1, peers)
    def _(k):
        pl.semaphore_signal(barrier, inc=1, device_id=place(peer(k)), device_id_type=pl.DeviceIdType.MESH)

    pl.semaphore_wait(barrier, peers)

    def to_core(k):
        at = peer(k)
        return pltpu.make_async_remote_copy(
            src_ref=partial.at[1 - ta, at], dst_ref=landed.at[at], send_sem=core_send.at[lax.rem(k, peers)],
            recv_sem=core_recv.at[lax.rem(k, peers)], device_id=other, device_id_type=pl.DeviceIdType.MESH)

    def to_peer(k):
        at = peer(k)
        return pltpu.make_async_remote_copy(
            src_ref=summed.at[at], dst_ref=arrived.at[k], send_sem=peer_send.at[k],
            recv_sem=peer_recv.at[k], device_id=place(at), device_id_type=pl.DeviceIdType.MESH)

    def stat_to(k):
        return pltpu.make_async_remote_copy(
            src_ref=stats, dst_ref=gathered.at[me], send_sem=stat_send.at[k],
            recv_sem=stat_recv.at[k], device_id=place(peer(k)), device_id_type=pl.DeviceIdType.MESH)

    @pl.loop(1, peers + 1)
    def _(k):
        to_core(k).start()

    @pl.loop(1, peers)
    def _(k):
        at = peer(k)
        to_core(k).wait_recv()
        summed[at] = (partial[ta, at].astype(jnp.float32) + landed[at].astype(jnp.float32)).astype(summed.dtype)
        to_peer(k).start()

    to_core(peers).wait_recv()
    new_weight[...] = partial[ta, me].astype(jnp.float32) + landed[me].astype(jnp.float32)

    @pl.loop(1, peers)
    def _(k):
        to_peer(k).wait_recv()
        new_weight[...] += arrived[k].astype(jnp.float32)

    total = new_weight[...]
    squares = jnp.sum(jnp.sum(total * total, axis=1, keepdims=True), axis=0, keepdims=True)
    lane = lax.broadcasted_iota(jnp.int32, stat_out.shape, 1)
    stat_out[...] = jnp.where(lane == 0, squares, local_loss[...])
    pair = pltpu.make_async_remote_copy(
        src_ref=stat_out, dst_ref=stat_in, send_sem=pair_sem.at[0], recv_sem=pair_sem.at[1],
        device_id=other, device_id_type=pl.DeviceIdType.MESH)
    pair.start()
    pair.wait()
    stats[...] = stat_out[...] + stat_in[...]
    gathered[me] = stats[...]

    @pl.loop(1, peers)
    def _(k):
        stat_to(k).start()

    @pl.loop(1, peers)
    def _(k):
        stat_to(k).wait_recv()

    both = jnp.sum(gathered[...], axis=0)
    norm = jnp.sqrt(both[0:1, 0:1])
    loss[...] = both[0:1, 1:2]
    clip = jnp.minimum(1.0, clip_norm / (norm + 1e-06))
    new_weight[...] = weight[...] - learn_rate * clip * new_weight[...]

    @pl.loop(1, peers)
    def _(k):
        to_core(k).wait_send()
        to_peer(k).wait_send()
        stat_to(k).wait_send()

    to_core(peers).wait_send()


def reduce_and_update(local_grad, local_loss, weight_rows):
    owned, classes = weight_rows.shape
    peers = lax.axis_size(("ha", "wa"))
    partial = local_grad.reshape(2, peers, owned, classes)
    vmem = pl.BlockSpec(memory_space=pltpu.VMEM)
    dma = pltpu.SemaphoreType.DMA
    slots = pltpu.VMEM((peers, owned, classes), local_grad.dtype)
    return pl.pallas_call(
        functools.partial(reduce_kernel, peers),
        in_specs=[vmem] * 3,
        out_specs=[vmem] * 2,
        out_shape=[
            jax.ShapeDtypeStruct((owned, classes), jnp.float32),
            jax.ShapeDtypeStruct((1, 1), jnp.float32),
        ],
        scratch_shapes=[slots, slots, slots]
        + [pltpu.VMEM((8, 128), jnp.float32)] * 3
        + [pltpu.VMEM((peers, 8, 128), jnp.float32)]
        + [dma((peers,))] * 6
        + [dma((2,))],
        compiler_params=pltpu.CompilerParams(collective_id=0, has_side_effects=True),
    )(partial, local_loss, weight_rows)


def local(features, teacher, head_weight):
    features, teacher = (jnp.transpose(array, (0, 2, 3, 1, 4)) for array in (features, teacher))
    batch, rows, columns, frames, width = features.shape
    classes = teacher.shape[-1]
    per_batch = columns * frames
    tokens = batch * per_batch
    ta, ha, wa = (lax.axis_index(axis) for axis in AXES)
    row, halo = exchange_halo(teacher)
    pool = pool_weights(columns, frames)
    frame_at = ta * frames + jnp.arange(frames, dtype=jnp.int32)
    row_at = ha * rows + jnp.arange(rows, dtype=jnp.int32)
    column_at = wa * columns + jnp.arange(columns, dtype=jnp.int32)

    def edge_count(position, length):
        return 3.0 - (position == 0).astype(jnp.float32) - (position == length - 1).astype(jnp.float32)

    own_clip = clip_of(column_at)
    left_ok = (column_at > 0) & (clip_of(column_at - 1) == own_clip)
    right_ok = (column_at < columns * lax.axis_size("wa") - 1) & (clip_of(column_at + 1) == own_clip)
    counts = (
        edge_count(row_at, rows * lax.axis_size("ha"))[:, None, None, None]
        * (1.0 + left_ok.astype(jnp.float32) + right_ok.astype(jnp.float32))[None, None, :, None]
        * edge_count(frame_at, frames * lax.axis_size("ta"))[None, None, None]
    )
    inverse = jnp.broadcast_to(1.0 / counts, (rows, batch, columns, frames)).reshape(rows, tokens, 1)
    flags = jnp.stack([(ha == 1), (ha == 0)]).astype(jnp.float32)
    head_bf = head_weight.astype(jnp.bfloat16)
    lag = lambda i: (0, jnp.maximum(i - 2, 0), 0, 0, 0)
    whole = lambda i: (0, 0)
    feature_grad, local_grad, loss = pl.pallas_call(
        functools.partial(fused_kernel, rows),
        grid=(rows + 2,),
        in_specs=[
            pl.BlockSpec(memory_space=pltpu.SMEM),
            pl.BlockSpec((batch, 1, columns, frames, classes), lambda i: (0, jnp.clip(i - 1, 0, rows - 1), 0, 0, 0)),
            pl.BlockSpec(row.shape, lambda i: (0, 0, 0, 0, 0)),
            pl.BlockSpec((batch, 1) + halo.shape[2:], lambda i: (0, jnp.where(i == 0, rows, i - 1), 0, 0)),
            pl.BlockSpec((batch, 1, columns, frames, width), lag),
            pl.BlockSpec(pool.shape, whole),
            pl.BlockSpec((1, tokens, 1), lambda i: (jnp.maximum(i - 2, 0), 0, 0)),
            pl.BlockSpec(head_bf.shape, whole),
        ],
        out_specs=[
            pl.BlockSpec((batch, 1, columns, frames, width), lag),
            pl.BlockSpec((width, classes), whole),
            pl.BlockSpec((1, 1), whole),
        ],
        out_shape=[
            jax.ShapeDtypeStruct(features.shape, features.dtype),
            jax.ShapeDtypeStruct((width, classes), jnp.bfloat16),
            jax.ShapeDtypeStruct((1, 1), jnp.float32),
        ],
        scratch_shapes=[
            pltpu.VMEM((3, tokens, classes), jnp.float32),
            pltpu.VMEM((rows * tokens, classes), jnp.bfloat16),
            pltpu.VMEM((rows * tokens, width), jnp.bfloat16),
        ],
        compiler_params=pltpu.CompilerParams(vmem_limit_bytes=60 * 1024 * 1024),
    )(flags, teacher, row, halo, features, pool, inverse, head_bf)
    feature_grad = jnp.transpose(feature_grad, (0, 3, 1, 2, 4))
    owned = width // lax.axis_size(AXES)
    weight_rows = lax.dynamic_slice_in_dim(head_weight, lax.axis_index(AXES) * owned, owned, 0)
    new_weight, loss = reduce_and_update(local_grad, loss, weight_rows)
    return feature_grad, loss[0, 0], new_weight


def solution(mesh):
    assert mesh.shape["ta"] == 2 and mesh.shape["ha"] == 2
    placed = (P(None, "ta", "ha", "wa", None), P(None, "ta", "ha", "wa", None), P())
    return jax.shard_map(
        local,
        mesh=mesh,
        in_specs=placed,
        out_specs=(P(None, "ta", "ha", "wa", None), P(), P(AXES, None)),
        check_vma=False,
    )
```

```python
import functools
import math

import jax
import jax.numpy as jnp
from jax import lax
from jax.experimental import pallas as pl
from jax.experimental.pallas import tpu as pltpu
from jax.sharding import PartitionSpec as P

WW = 14
WV = 28
AXES = ("ta", "ha", "wa")

sharpness_divisor = 2.0
learn_rate = 0.1
clip_norm = 1000.0
EXP2_SCALE = math.log2(math.e) / sharpness_divisor


def clip_of(columns):
    return (columns + WV - WW // 2) // WV


def exchange_halo(teacher):
    batch, rows, columns, frames, classes = teacher.shape
    ta, ha = lax.axis_index("ta"), lax.axis_index("ha")
    swap = [(0, 1), (1, 0)]
    count = lax.axis_size("wa")
    forward = [(i, i + 1) for i in range(count - 1)]
    backward = [(target, source) for source, target in forward]

    def facing_frame(cells):
        facing = lax.broadcasted_iota(jnp.int32, cells.shape, cells.ndim - 2) == jnp.where(ta == 0, frames - 1, 0)
        return jnp.sum(jnp.where(facing, cells, jnp.zeros_like(cells)), axis=-2)

    wa = lax.axis_index("wa")
    facing_row = jnp.where(ha == 0, rows - 1, 0)

    def column(at):
        return lax.dynamic_slice_in_dim(teacher, at, 1, 2)[:, :, 0]

    left = lax.ppermute(column(jnp.minimum(wa + columns - 1, columns - 1)), "wa", forward)
    right = lax.ppermute(column(jnp.maximum(-wa, 0)), "wa", backward)
    row = lax.ppermute(lax.dynamic_slice_in_dim(teacher, facing_row, 1, 1), "ha", swap)
    frame = lax.ppermute(facing_frame(teacher), "ta", swap)
    sides = jnp.concatenate([left, right], 2)
    corner = lax.ppermute(lax.dynamic_slice_in_dim(sides, facing_row, 1, 1), "ha", swap)
    sides = jnp.concatenate([sides, corner], 1)
    edges = [facing_frame(part) for part in (row[:, 0], sides[:, :, :frames], sides[:, :, frames:])]
    edges = lax.ppermute(jnp.concatenate(edges, 1), "ta", swap)
    frame = jnp.concatenate([frame, edges[:, None, :columns]], 1)
    frame_left = edges[:, columns : columns + rows + 1, None]
    frame_right = edges[:, columns + rows + 1 :, None]
    return row, sides, jnp.concatenate([frame, frame_left, frame_right], 2)


def pool_weights(columns, frames):
    ta, wa = lax.axis_index("ta"), lax.axis_index("wa")
    grid_wide = columns * lax.axis_size("wa")
    out = jnp.arange(columns * frames, dtype=jnp.int32)
    out_col, out_frame = out // frames, out % frames
    every = jnp.arange(frames, dtype=jnp.int32)
    cols = jnp.arange(columns, dtype=jnp.int32)
    next_frame = jnp.where(ta == 0, frames, -1)
    src_col = jnp.concatenate([out_col, 0 * every - 1, 0 * every + columns, cols, jnp.array([-1, columns], jnp.int32)])
    src_frame = jnp.concatenate([out_frame, every, every, jnp.full((columns + 2,), 1, jnp.int32) * next_frame])
    out_at, src_at = wa * columns + out_col, wa * columns + src_col
    near = (jnp.abs(out_frame[:, None] - src_frame[None]) <= 1) & (jnp.abs(out_col[:, None] - src_col[None]) <= 1)
    inside = (src_at >= 0) & (src_at < grid_wide)
    same = clip_of(out_at)[:, None] == clip_of(src_at)[None]
    return (near & inside[None] & same).astype(jnp.bfloat16)


def fused_kernel(rows, flags, own, halo_row, sides, ahead, feats, pool, inverse, head, grad_out, head_grad, loss, sums, slopes, feat_keep):
    step = pl.program_id(0)
    batch, _, columns, frames, width = feats.shape
    per_batch = columns * frames
    tokens = batch * per_batch
    classes = head.shape[1]

    def planar(slot, cells_of, scale=None):
        for b in range(batch):
            cells = jnp.concatenate([cells_of(b).reshape(per_batch, classes), sides[b, 0], ahead[b, 0]], axis=0)
            part = jnp.dot(pool[...], cells, preferred_element_type=jnp.float32)
            sums[slot, b * per_batch : (b + 1) * per_batch] = part if scale is None else part * scale

    @pl.when(step == 0)
    def _():
        loss[...] = jnp.zeros_like(loss)
        planar(rows % 3, lambda b: halo_row[b, 0], flags[0])

    @pl.when((step > 0) & (step <= rows))
    def _():
        planar(lax.rem(step - 1, 3), lambda b: own[b, 0])

    @pl.when(step == rows + 1)
    def _():
        planar(rows % 3, lambda b: halo_row[b, 0], flags[1])

    @pl.when(step > 1)
    def _():
        at = step - 2
        features = feats[...].reshape(tokens, width)
        student = jnp.dot(features, head[...], preferred_element_type=jnp.float32)
        pooled = (sums[0] + sums[1] + sums[2]) * inverse[0]
        teach = (pooled - jnp.max(pooled, -1, keepdims=True)) * EXP2_SCALE
        learn = (student - jnp.max(student, -1, keepdims=True)) * EXP2_SCALE
        teach_exp, learn_exp = jnp.exp2(teach), jnp.exp2(learn)
        teach_sum = jnp.sum(teach_exp, -1, keepdims=True)
        learn_sum = jnp.sum(learn_exp, -1, keepdims=True)
        cross = jnp.sum(teach_exp * (teach - learn), -1, keepdims=True)
        kl = math.log(2.0) * cross / teach_sum + jnp.log(learn_sum) - jnp.log(teach_sum)
        loss[...] += sharpness_divisor * sharpness_divisor * jnp.sum(kl, axis=0, keepdims=True)
        slope = learn_exp * (sharpness_divisor / learn_sum) - teach_exp * (sharpness_divisor / teach_sum)
        slope = slope.astype(jnp.bfloat16)
        grad = lax.dot_general(slope, head[...], (((1,), (1,)), ((), ())), preferred_element_type=jnp.float32)
        grad_out[...] = grad.astype(grad_out.dtype).reshape(grad_out.shape)
        where = pl.ds(pl.multiple_of(at * tokens, 16), tokens)
        slopes[where] = slope
        feat_keep[where] = features

    @pl.when(step == rows + 1)
    def _():
        chunk = 256

        @pl.loop(0, width // chunk)
        def _(i):
            part = pl.ds(pl.multiple_of(i * chunk, chunk), chunk)
            head_grad[part] = lax.dot_general(
                feat_keep[:, part], slopes[...], (((0,), (0,)), ((), ())), preferred_element_type=jnp.float32
            ).astype(head_grad.dtype)


def reduce_kernel(peers, partial, local_loss, weight, new_weight, loss, landed, summed, arrived, stats, stat_in, stat_out, gathered,
                  core_send, core_recv, peer_send, peer_recv, stat_send, stat_recv, pair_sem):
    ta, ha, wa = (lax.axis_index(axis) for axis in AXES)
    per_row = lax.axis_size("wa")
    me = ha * per_row + wa
    other = {"ta": 1 - ta}

    def peer(k):
        return lax.rem(me + k, peers)

    def place(at):
        return {"ha": at // per_row, "wa": lax.rem(at, per_row)}

    barrier = pltpu.get_barrier_semaphore()
    pl.semaphore_signal(barrier, inc=1, device_id=other, device_id_type=pl.DeviceIdType.MESH)

    @pl.loop(1, peers)
    def _(k):
        pl.semaphore_signal(barrier, inc=1, device_id=place(peer(k)), device_id_type=pl.DeviceIdType.MESH)

    pl.semaphore_wait(barrier, peers)

    def to_core(k):
        at = peer(k)
        return pltpu.make_async_remote_copy(
            src_ref=partial.at[1 - ta, at], dst_ref=landed.at[at], send_sem=core_send.at[lax.rem(k, peers)],
            recv_sem=core_recv.at[lax.rem(k, peers)], device_id=other, device_id_type=pl.DeviceIdType.MESH)

    def to_peer(k):
        at = peer(k)
        return pltpu.make_async_remote_copy(
            src_ref=summed.at[at], dst_ref=arrived.at[k], send_sem=peer_send.at[k],
            recv_sem=peer_recv.at[k], device_id=place(at), device_id_type=pl.DeviceIdType.MESH)

    def stat_to(k):
        return pltpu.make_async_remote_copy(
            src_ref=stats, dst_ref=gathered.at[me], send_sem=stat_send.at[k],
            recv_sem=stat_recv.at[k], device_id=place(peer(k)), device_id_type=pl.DeviceIdType.MESH)

    @pl.loop(1, peers + 1)
    def _(k):
        to_core(k).start()

    @pl.loop(1, peers)
    def _(k):
        at = peer(k)
        to_core(k).wait_recv()
        summed[at] = (partial[ta, at].astype(jnp.float32) + landed[at].astype(jnp.float32)).astype(summed.dtype)
        to_peer(k).start()

    to_core(peers).wait_recv()
    new_weight[...] = partial[ta, me].astype(jnp.float32) + landed[me].astype(jnp.float32)

    @pl.loop(1, peers)
    def _(k):
        to_peer(k).wait_recv()
        new_weight[...] += arrived[k].astype(jnp.float32)

    total = new_weight[...]
    squares = jnp.sum(jnp.sum(total * total, axis=1, keepdims=True), axis=0, keepdims=True)
    lane = lax.broadcasted_iota(jnp.int32, stat_out.shape, 1)
    stat_out[...] = jnp.where(lane == 0, squares, local_loss[...])
    pair = pltpu.make_async_remote_copy(
        src_ref=stat_out, dst_ref=stat_in, send_sem=pair_sem.at[0], recv_sem=pair_sem.at[1],
        device_id=other, device_id_type=pl.DeviceIdType.MESH)
    pair.start()
    pair.wait()
    stats[...] = stat_out[...] + stat_in[...]
    gathered[me] = stats[...]

    @pl.loop(1, peers)
    def _(k):
        stat_to(k).start()

    @pl.loop(1, peers)
    def _(k):
        stat_to(k).wait_recv()

    both = jnp.sum(gathered[...], axis=0)
    norm = jnp.sqrt(both[0:1, 0:1])
    loss[...] = both[0:1, 1:2]
    clip = jnp.minimum(1.0, clip_norm / (norm + 1e-06))
    new_weight[...] = weight[...] - learn_rate * clip * new_weight[...]

    @pl.loop(1, peers)
    def _(k):
        to_core(k).wait_send()
        to_peer(k).wait_send()
        stat_to(k).wait_send()

    to_core(peers).wait_send()


def reduce_and_update(local_grad, local_loss, weight_rows):
    owned, classes = weight_rows.shape
    peers = lax.axis_size(("ha", "wa"))
    partial = local_grad.reshape(2, peers, owned, classes)
    vmem = pl.BlockSpec(memory_space=pltpu.VMEM)
    dma = pltpu.SemaphoreType.DMA
    slots = pltpu.VMEM((peers, owned, classes), local_grad.dtype)
    return pl.pallas_call(
        functools.partial(reduce_kernel, peers),
        in_specs=[vmem] * 3,
        out_specs=[vmem] * 2,
        out_shape=[
            jax.ShapeDtypeStruct((owned, classes), jnp.float32),
            jax.ShapeDtypeStruct((1, 1), jnp.float32),
        ],
        scratch_shapes=[slots, slots, slots]
        + [pltpu.VMEM((8, 128), jnp.float32)] * 3
        + [pltpu.VMEM((peers, 8, 128), jnp.float32)]
        + [dma((peers,))] * 6
        + [dma((2,))],
        compiler_params=pltpu.CompilerParams(collective_id=0, has_side_effects=True),
    )(partial, local_loss, weight_rows)


def local(features, teacher, head_weight):
    features, teacher = (jnp.transpose(array, (0, 2, 3, 1, 4)) for array in (features, teacher))
    batch, rows, columns, frames, width = features.shape
    classes = teacher.shape[-1]
    per_batch = columns * frames
    tokens = batch * per_batch
    ta, ha, wa = (lax.axis_index(axis) for axis in AXES)
    row, sides, ahead = exchange_halo(teacher)
    pool = pool_weights(columns, frames)
    frame_at = ta * frames + jnp.arange(frames, dtype=jnp.int32)
    row_at = ha * rows + jnp.arange(rows, dtype=jnp.int32)
    column_at = wa * columns + jnp.arange(columns, dtype=jnp.int32)

    def edge_count(position, length):
        return 3.0 - (position == 0).astype(jnp.float32) - (position == length - 1).astype(jnp.float32)

    own_clip = clip_of(column_at)
    left_ok = (column_at > 0) & (clip_of(column_at - 1) == own_clip)
    right_ok = (column_at < columns * lax.axis_size("wa") - 1) & (clip_of(column_at + 1) == own_clip)
    counts = (
        edge_count(row_at, rows * lax.axis_size("ha"))[:, None, None, None]
        * (1.0 + left_ok.astype(jnp.float32) + right_ok.astype(jnp.float32))[None, None, :, None]
        * edge_count(frame_at, frames * lax.axis_size("ta"))[None, None, None]
    )
    inverse = jnp.broadcast_to(1.0 / counts, (rows, batch, columns, frames)).reshape(rows, tokens, 1)
    flags = jnp.stack([(ha == 1), (ha == 0)]).astype(jnp.float32)
    head_bf = head_weight.astype(jnp.bfloat16)
    lag = lambda i: (0, jnp.maximum(i - 2, 0), 0, 0, 0)
    beside = lambda i: (0, jnp.where(i == 0, rows, i - 1), 0, 0)
    whole = lambda i: (0, 0)
    feature_grad, local_grad, loss = pl.pallas_call(
        functools.partial(fused_kernel, rows),
        grid=(rows + 2,),
        in_specs=[
            pl.BlockSpec(memory_space=pltpu.SMEM),
            pl.BlockSpec((batch, 1, columns, frames, classes), lambda i: (0, jnp.clip(i - 1, 0, rows - 1), 0, 0, 0)),
            pl.BlockSpec(row.shape, lambda i: (0, 0, 0, 0, 0)),
            pl.BlockSpec((batch, 1) + sides.shape[2:], beside),
            pl.BlockSpec((batch, 1) + ahead.shape[2:], beside),
            pl.BlockSpec((batch, 1, columns, frames, width), lag),
            pl.BlockSpec(pool.shape, whole),
            pl.BlockSpec((1, tokens, 1), lambda i: (jnp.maximum(i - 2, 0), 0, 0)),
            pl.BlockSpec(head_bf.shape, whole),
        ],
        out_specs=[
            pl.BlockSpec((batch, 1, columns, frames, width), lag),
            pl.BlockSpec((width, classes), whole),
            pl.BlockSpec((1, 1), whole),
        ],
        out_shape=[
            jax.ShapeDtypeStruct(features.shape, features.dtype),
            jax.ShapeDtypeStruct((width, classes), jnp.bfloat16),
            jax.ShapeDtypeStruct((1, 1), jnp.float32),
        ],
        scratch_shapes=[
            pltpu.VMEM((3, tokens, classes), jnp.float32),
            pltpu.VMEM((rows * tokens, classes), jnp.bfloat16),
            pltpu.VMEM((rows * tokens, width), jnp.bfloat16),
        ],
        compiler_params=pltpu.CompilerParams(vmem_limit_bytes=60 * 1024 * 1024),
    )(flags, teacher, row, sides, ahead, features, pool, inverse, head_bf)
    feature_grad = jnp.transpose(feature_grad, (0, 3, 1, 2, 4))
    owned = width // lax.axis_size(AXES)
    weight_rows = lax.dynamic_slice_in_dim(head_weight, lax.axis_index(AXES) * owned, owned, 0)
    new_weight, loss = reduce_and_update(local_grad, loss, weight_rows)
    return feature_grad, loss[0, 0], new_weight


def solution(mesh):
    assert mesh.shape["ta"] == 2 and mesh.shape["ha"] == 2
    placed = (P(None, "ta", "ha", "wa", None), P(None, "ta", "ha", "wa", None), P())
    return jax.shard_map(
        local,
        mesh=mesh,
        in_specs=placed,
        out_specs=(P(None, "ta", "ha", "wa", None), P(), P(AXES, None)),
        check_vma=False,
    )
```

```python
import functools
import math

import jax
import jax.numpy as jnp
from jax import lax
from jax.experimental import pallas as pl
from jax.experimental.pallas import tpu as pltpu
from jax.sharding import PartitionSpec as P

WW = 14
WV = 28
AXES = ("ta", "ha", "wa")

sharpness_divisor = 2.0
learn_rate = 0.1
clip_norm = 1000.0
EXP2_SCALE = math.log2(math.e) / sharpness_divisor


def clip_of(columns):
    return (columns + WV - WW // 2) // WV


def exchange_halo(teacher):
    batch, rows, columns, frames, classes = teacher.shape
    ta, ha = lax.axis_index("ta"), lax.axis_index("ha")
    swap = [(0, 1), (1, 0)]
    count = lax.axis_size("wa")
    forward = [(i, i + 1) for i in range(count - 1)]
    backward = [(target, source) for source, target in forward]

    def facing_frame(cells):
        facing = lax.broadcasted_iota(jnp.int32, cells.shape, cells.ndim - 2) == jnp.where(ta == 0, frames - 1, 0)
        return jnp.sum(jnp.where(facing, cells, jnp.zeros_like(cells)), axis=-2)

    wa = lax.axis_index("wa")
    facing_row = jnp.where(ha == 0, rows - 1, 0)

    def column(at):
        return lax.dynamic_slice_in_dim(teacher, at, 1, 2)[:, :, 0]

    left = lax.ppermute(column(jnp.minimum(wa + columns - 1, columns - 1)), "wa", forward)
    right = lax.ppermute(column(jnp.maximum(-wa, 0)), "wa", backward)
    row = lax.ppermute(lax.dynamic_slice_in_dim(teacher, facing_row, 1, 1), "ha", swap)
    frame = lax.ppermute(facing_frame(teacher), "ta", swap)
    sides = jnp.concatenate([left, right], 2)
    corner = lax.ppermute(lax.dynamic_slice_in_dim(sides, facing_row, 1, 1), "ha", swap)
    sides = jnp.concatenate([sides, corner], 1)
    edges = [facing_frame(part) for part in (row[:, 0], sides[:, :, :frames], sides[:, :, frames:])]
    edges = lax.ppermute(jnp.concatenate(edges, 1), "ta", swap)
    frame = jnp.concatenate([frame, edges[:, None, :columns]], 1)
    frame_left = edges[:, columns : columns + rows + 1, None]
    frame_right = edges[:, columns + rows + 1 :, None]
    return row, sides, jnp.concatenate([frame, frame_left, frame_right], 2)


def pool_weights(columns, frames):
    ta, wa = lax.axis_index("ta"), lax.axis_index("wa")
    grid_wide = columns * lax.axis_size("wa")
    out = jnp.arange(columns * frames, dtype=jnp.int32)
    out_col, out_frame = out // frames, out % frames
    every = jnp.arange(frames, dtype=jnp.int32)
    cols = jnp.arange(columns, dtype=jnp.int32)
    next_frame = jnp.where(ta == 0, frames, -1)
    src_col = jnp.concatenate([out_col, 0 * every - 1, 0 * every + columns, cols, jnp.array([-1, columns], jnp.int32)])
    src_frame = jnp.concatenate([out_frame, every, every, jnp.full((columns + 2,), 1, jnp.int32) * next_frame])
    out_at, src_at = wa * columns + out_col, wa * columns + src_col
    near = (jnp.abs(out_frame[:, None] - src_frame[None]) <= 1) & (jnp.abs(out_col[:, None] - src_col[None]) <= 1)
    inside = (src_at >= 0) & (src_at < grid_wide)
    same = clip_of(out_at)[:, None] == clip_of(src_at)[None]
    return (near & inside[None] & same).astype(jnp.bfloat16)


def fused_kernel(rows, flags, own, halo_row, sides, ahead, feats, pool, inverse, head, grad_out, head_grad, loss, sums, slopes, feat_keep):
    step = pl.program_id(0)
    batch, _, columns, frames, width = feats.shape
    per_batch = columns * frames
    tokens = batch * per_batch
    classes = head.shape[1]

    def planar(slot, cells_of, scale=None):
        for b in range(batch):
            cells = jnp.concatenate([cells_of(b).reshape(per_batch, classes), sides[b, 0], ahead[b, 0]], axis=0)
            part = jnp.dot(pool[...], cells, preferred_element_type=jnp.float32)
            sums[slot, b * per_batch : (b + 1) * per_batch] = part if scale is None else part * scale

    @pl.when(step == 0)
    def _():
        loss[...] = jnp.zeros_like(loss)
        planar(rows % 3, lambda b: halo_row[b, 0], flags[0])

    @pl.when((step > 0) & (step <= rows))
    def _():
        planar(lax.rem(step - 1, 3), lambda b: own[b, 0])

    @pl.when(step == rows + 1)
    def _():
        planar(rows % 3, lambda b: halo_row[b, 0], flags[1])

    @pl.when(step > 1)
    def _():
        at = step - 2
        features = feats[...].reshape(tokens, width)
        student = jnp.dot(features, head[...], preferred_element_type=jnp.float32)
        pooled = (sums[0] + sums[1] + sums[2]) * (inverse[...] * flags[2 + at])
        teach = (pooled - jnp.max(pooled, -1, keepdims=True)) * EXP2_SCALE
        learn = (student - jnp.max(student, -1, keepdims=True)) * EXP2_SCALE
        teach_exp, learn_exp = jnp.exp2(teach), jnp.exp2(learn)
        teach_sum = jnp.sum(teach_exp, -1, keepdims=True)
        learn_sum = jnp.sum(learn_exp, -1, keepdims=True)
        cross = jnp.sum(teach_exp * (teach - learn), -1, keepdims=True)
        kl = math.log(2.0) * cross / teach_sum + jnp.log(learn_sum) - jnp.log(teach_sum)
        loss[...] += sharpness_divisor * sharpness_divisor * jnp.sum(kl, axis=0, keepdims=True)
        slope = learn_exp * (sharpness_divisor / learn_sum) - teach_exp * (sharpness_divisor / teach_sum)
        slope = slope.astype(jnp.bfloat16)
        grad = lax.dot_general(slope, head[...], (((1,), (1,)), ((), ())), preferred_element_type=jnp.float32)
        grad_out[...] = grad.astype(grad_out.dtype).reshape(grad_out.shape)
        where = pl.ds(pl.multiple_of(at * tokens, 16), tokens)
        slopes[where] = slope
        feat_keep[where] = features

    @pl.when(step == rows + 1)
    def _():
        chunk = 256

        @pl.loop(0, width // chunk)
        def _(i):
            part = pl.ds(pl.multiple_of(i * chunk, chunk), chunk)
            head_grad[part] = lax.dot_general(
                feat_keep[:, part], slopes[...], (((0,), (0,)), ((), ())), preferred_element_type=jnp.float32
            ).astype(head_grad.dtype)


def reduce_kernel(peers, partial, local_loss, weight, new_weight, loss, landed, summed, arrived, stats, stat_in, stat_out, gathered,
                  core_send, core_recv, peer_send, peer_recv, stat_send, stat_recv, pair_sem):
    ta, ha, wa = (lax.axis_index(axis) for axis in AXES)
    per_row = lax.axis_size("wa")
    me = ha * per_row + wa
    other = {"ta": 1 - ta}

    def peer(k):
        return lax.rem(me + k, peers)

    def place(at):
        return {"ha": at // per_row, "wa": lax.rem(at, per_row)}

    barrier = pltpu.get_barrier_semaphore()
    pl.semaphore_signal(barrier, inc=1, device_id=other, device_id_type=pl.DeviceIdType.MESH)

    @pl.loop(1, peers)
    def _(k):
        pl.semaphore_signal(barrier, inc=1, device_id=place(peer(k)), device_id_type=pl.DeviceIdType.MESH)

    pl.semaphore_wait(barrier, peers)

    def to_core(k):
        at = peer(k)
        return pltpu.make_async_remote_copy(
            src_ref=partial.at[1 - ta, at], dst_ref=landed.at[at], send_sem=core_send.at[lax.rem(k, peers)],
            recv_sem=core_recv.at[lax.rem(k, peers)], device_id=other, device_id_type=pl.DeviceIdType.MESH)

    def to_peer(k):
        at = peer(k)
        return pltpu.make_async_remote_copy(
            src_ref=summed.at[at], dst_ref=arrived.at[k], send_sem=peer_send.at[k],
            recv_sem=peer_recv.at[k], device_id=place(at), device_id_type=pl.DeviceIdType.MESH)

    def stat_to(k):
        return pltpu.make_async_remote_copy(
            src_ref=stats, dst_ref=gathered.at[me], send_sem=stat_send.at[k],
            recv_sem=stat_recv.at[k], device_id=place(peer(k)), device_id_type=pl.DeviceIdType.MESH)

    @pl.loop(1, peers + 1)
    def _(k):
        to_core(k).start()

    @pl.loop(1, peers)
    def _(k):
        at = peer(k)
        to_core(k).wait_recv()
        summed[at] = (partial[ta, at].astype(jnp.float32) + landed[at].astype(jnp.float32)).astype(summed.dtype)
        to_peer(k).start()

    to_core(peers).wait_recv()
    new_weight[...] = partial[ta, me].astype(jnp.float32) + landed[me].astype(jnp.float32)

    @pl.loop(1, peers)
    def _(k):
        to_peer(k).wait_recv()
        new_weight[...] += arrived[k].astype(jnp.float32)

    total = new_weight[...]
    squares = jnp.sum(jnp.sum(total * total, axis=1, keepdims=True), axis=0, keepdims=True)
    lane = lax.broadcasted_iota(jnp.int32, stat_out.shape, 1)
    stat_out[...] = jnp.where(lane == 0, squares, local_loss[...])
    pair = pltpu.make_async_remote_copy(
        src_ref=stat_out, dst_ref=stat_in, send_sem=pair_sem.at[0], recv_sem=pair_sem.at[1],
        device_id=other, device_id_type=pl.DeviceIdType.MESH)
    pair.start()
    pair.wait()
    stats[...] = stat_out[...] + stat_in[...]
    gathered[me] = stats[...]

    @pl.loop(1, peers)
    def _(k):
        stat_to(k).start()

    @pl.loop(1, peers)
    def _(k):
        stat_to(k).wait_recv()

    both = jnp.sum(gathered[...], axis=0)
    norm = jnp.sqrt(both[0:1, 0:1])
    loss[...] = both[0:1, 1:2]
    clip = jnp.minimum(1.0, clip_norm / (norm + 1e-06))
    new_weight[...] = weight[...] - learn_rate * clip * new_weight[...]

    @pl.loop(1, peers)
    def _(k):
        to_core(k).wait_send()
        to_peer(k).wait_send()
        stat_to(k).wait_send()

    to_core(peers).wait_send()


def reduce_and_update(local_grad, local_loss, weight_rows):
    owned, classes = weight_rows.shape
    peers = lax.axis_size(("ha", "wa"))
    partial = local_grad.reshape(2, peers, owned, classes)
    vmem = pl.BlockSpec(memory_space=pltpu.VMEM)
    dma = pltpu.SemaphoreType.DMA
    slots = pltpu.VMEM((peers, owned, classes), local_grad.dtype)
    return pl.pallas_call(
        functools.partial(reduce_kernel, peers),
        in_specs=[vmem] * 3,
        out_specs=[vmem] * 2,
        out_shape=[
            jax.ShapeDtypeStruct((owned, classes), jnp.float32),
            jax.ShapeDtypeStruct((1, 1), jnp.float32),
        ],
        scratch_shapes=[slots, slots, slots]
        + [pltpu.VMEM((8, 128), jnp.float32)] * 3
        + [pltpu.VMEM((peers, 8, 128), jnp.float32)]
        + [dma((peers,))] * 6
        + [dma((2,))],
        compiler_params=pltpu.CompilerParams(collective_id=0, has_side_effects=True),
    )(partial, local_loss, weight_rows)


def local(features, teacher, head_weight):
    features, teacher = (jnp.transpose(array, (0, 2, 3, 1, 4)) for array in (features, teacher))
    batch, rows, columns, frames, width = features.shape
    classes = teacher.shape[-1]
    per_batch = columns * frames
    tokens = batch * per_batch
    ta, ha, wa = (lax.axis_index(axis) for axis in AXES)
    row, sides, ahead = exchange_halo(teacher)
    pool = pool_weights(columns, frames)
    frame_at = ta * frames + jnp.arange(frames, dtype=jnp.int32)
    row_at = ha * rows + jnp.arange(rows, dtype=jnp.int32)
    column_at = wa * columns + jnp.arange(columns, dtype=jnp.int32)

    def edge_count(position, length):
        return 3.0 - (position == 0).astype(jnp.float32) - (position == length - 1).astype(jnp.float32)

    own_clip = clip_of(column_at)
    left_ok = (column_at > 0) & (clip_of(column_at - 1) == own_clip)
    right_ok = (column_at < columns * lax.axis_size("wa") - 1) & (clip_of(column_at + 1) == own_clip)
    counts = (
        (1.0 + left_ok.astype(jnp.float32) + right_ok.astype(jnp.float32))[None, :, None]
        * edge_count(frame_at, frames * lax.axis_size("ta"))[None, None]
    )
    inverse = jnp.broadcast_to(1.0 / counts, (batch, columns, frames)).reshape(tokens, 1)
    flags = jnp.stack([(ha == 1), (ha == 0)]).astype(jnp.float32)
    flags = jnp.concatenate([flags, 1.0 / edge_count(row_at, rows * lax.axis_size("ha"))])
    head_bf = head_weight.astype(jnp.bfloat16)
    lag = lambda i: (0, jnp.maximum(i - 2, 0), 0, 0, 0)
    beside = lambda i: (0, jnp.where(i == 0, rows, i - 1), 0, 0)
    whole = lambda i: (0, 0)
    feature_grad, local_grad, loss = pl.pallas_call(
        functools.partial(fused_kernel, rows),
        grid=(rows + 2,),
        in_specs=[
            pl.BlockSpec(memory_space=pltpu.SMEM),
            pl.BlockSpec((batch, 1, columns, frames, classes), lambda i: (0, jnp.clip(i - 1, 0, rows - 1), 0, 0, 0)),
            pl.BlockSpec(row.shape, lambda i: (0, 0, 0, 0, 0)),
            pl.BlockSpec((batch, 1) + sides.shape[2:], beside),
            pl.BlockSpec((batch, 1) + ahead.shape[2:], beside),
            pl.BlockSpec((batch, 1, columns, frames, width), lag),
            pl.BlockSpec(pool.shape, whole),
            pl.BlockSpec((tokens, 1), whole),
            pl.BlockSpec(head_bf.shape, whole),
        ],
        out_specs=[
            pl.BlockSpec((batch, 1, columns, frames, width), lag),
            pl.BlockSpec((width, classes), whole),
            pl.BlockSpec((1, 1), whole),
        ],
        out_shape=[
            jax.ShapeDtypeStruct(features.shape, features.dtype),
            jax.ShapeDtypeStruct((width, classes), jnp.bfloat16),
            jax.ShapeDtypeStruct((1, 1), jnp.float32),
        ],
        scratch_shapes=[
            pltpu.VMEM((3, tokens, classes), jnp.float32),
            pltpu.VMEM((rows * tokens, classes), jnp.bfloat16),
            pltpu.VMEM((rows * tokens, width), jnp.bfloat16),
        ],
        compiler_params=pltpu.CompilerParams(vmem_limit_bytes=60 * 1024 * 1024),
    )(flags, teacher, row, sides, ahead, features, pool, inverse, head_bf)
    feature_grad = jnp.transpose(feature_grad, (0, 3, 1, 2, 4))
    owned = width // lax.axis_size(AXES)
    weight_rows = lax.dynamic_slice_in_dim(head_weight, lax.axis_index(AXES) * owned, owned, 0)
    new_weight, loss = reduce_and_update(local_grad, loss, weight_rows)
    return feature_grad, loss[0, 0], new_weight


def solution(mesh):
    assert mesh.shape["ta"] == 2 and mesh.shape["ha"] == 2
    placed = (P(None, "ta", "ha", "wa", None), P(None, "ta", "ha", "wa", None), P())
    return jax.shard_map(
        local,
        mesh=mesh,
        in_specs=placed,
        out_specs=(P(None, "ta", "ha", "wa", None), P(), P(AXES, None)),
        check_vma=False,
    )
```
